32 devices in a mesh: section: 2 (over y), channel: 4 (over x, core), block: 4 (over z).
Axes of the slice: x: 2, y: 2, z: 4, core: 2. Of those that a mesh axis runs over, the one named last changes fastest.
Arguments:
- env: bfloat16 [2, 16, 16, 512, 512], P('section', 'channel', 'block'), may hold values from -6 to 6
- site_tensor: bfloat16 [2, 4, 16, 512, 512], P('section', None, 'block'), may hold values from -0.25 to 0.25
- mpo: bfloat16 [2, 16, 16, 4], P('section'), may hold values from -2 to 2
- channel_mask: int32 [2, 16, 16], P('section'), may hold values 0 or 1
- block_mask: int32 [2, 4, 16], P('section', None, 'block'), may hold values 0 or 1
- state_charge: int32 [4], replicated, may hold values from 0 to 1, as said below
- psi: bfloat16 [2, 16, 512, 512], P('section', 'block'), may hold values from -0.0014648438 to 0.0014648438
Outputs:
- new_env: bfloat16 [2, 16, 16, 512, 512], P('section', 'channel', 'block')
- new_psi: bfloat16 [512, 2, 16, 512], P('channel', 'section', 'block')
The draws below stay inside these ranges and needn't reach their ends.
Inputs may be any that keep to these rules, and one draw needn't show every extreme that they name: `state_charge`: half of the 4 site states carry charge 0, the others charge 1.
All inputs are finite; a program needn't handle non-finite values. No bound on the sum of `channel_mask` or of `block_mask` on one device may be relied on, other than what follows from the above.
Results may differ from the reference program's by a relative error of at most 0.017.
Values may be sent and summed in bfloat16 or wider, within the bound.
No kernel may reach another device: no remote copies, remote signals or barrier semaphores. Data moves between devices by JAX's collectives and lax.ppermute only.
A program may use at most 192 MiB of HBM per device.

```python
import jax
import jax.numpy as jnp
from jax import lax

SDIM = 512
SECTORS = 16
CHAN = 16
STATES = 4
VECS = 2


def draw_state_charge(key, part):
    base_charge = (jnp.arange(STATES) % 2).astype(jnp.int32)
    return jax.random.permutation(key, base_charge)


def with_ends(values, key, least, top_value):
    longest = values.shape.index(max(values.shape))
    spots = []
    for shift in (0, 1):
        where = [jax.random.randint(jax.random.fold_in(key, axis), (), 0, length) for axis, length in enumerate(values.shape)]
        where[longest] = (where[longest] + shift) % values.shape[longest]
        spots.append(tuple(where))
    return values.at[spots[0]].set(least).at[spots[1]].set(top_value)


def block_scale(own_key, shape, cuts, smallest, high):
    loudness, own = 1.0, jax.random.fold_in(own_key, 6)
    for dim, shards_of in cuts:
        draws = jnp.exp(jax.random.uniform(jax.random.fold_in(own, dim), (shards_of,), jnp.float32, smallest / len(cuts), high / len(cuts)))
        loudness = loudness * jnp.repeat(draws, shape[dim] // shards_of).reshape([-1 if axis == dim else 1 for axis in range(len(shape))])
    return loudness


def centred(stream_key, shape, spread, limit, pieces=(), dtype=jnp.bfloat16):
    entries = spread * jax.random.normal(stream_key, shape, jnp.float32)
    if pieces:
        entries = entries * block_scale(stream_key, shape, pieces, -0.22, 0.18)
    return jnp.clip(entries, -limit, limit).astype(dtype)


def setup_inputs(seed: int = 0) -> dict:
    key_list = jax.random.split(jax.random.key(seed), 8)
    env = centred(key_list[0], (2, CHAN, SECTORS, SDIM, SDIM), 1.0, 6.0, ((0, 2), (1, 4), (2, 4)))
    site_tensor = centred(key_list[1], (2, STATES, SECTORS, SDIM, SDIM), SDIM ** -0.5, 0.25, ((0, 2), (2, 4)))
    mpo = centred(key_list[2], (2, CHAN, CHAN, STATES), (CHAN // 2) ** -0.5, 2.0, ((0, 2),))
    channel_mask = with_ends((jax.random.randint(key_list[3], (2, CHAN, CHAN), 0, 2) < 1).astype(jnp.int32), jax.random.fold_in(key_list[3], 1), 0, 1)
    block_mask = with_ends((jax.random.randint(key_list[4], (2, STATES, SECTORS), 0, 4) < 3).astype(jnp.int32), jax.random.fold_in(key_list[4], 1), 0, 1)
    state_charge = draw_state_charge(jax.random.fold_in(key_list[7], 71), 0)
    psi = centred(key_list[6], (VECS, SECTORS, SDIM, SDIM), (0.125 / SDIM), 0.0014648438, ((0, 2), (1, 4)))
    return dict(env=env, site_tensor=site_tensor, mpo=mpo, channel_mask=channel_mask, block_mask=block_mask, state_charge=state_charge, psi=psi)


def sector_env(weights, charge_label, env_q, site_q, mask_q):
    blended_environment = jnp.einsum("wvs,wab->vsab", weights, env_q.astype(jnp.float32)).astype(jnp.bfloat16)
    product = jnp.einsum("vsac,scb->vsab", blended_environment.astype(jnp.float32), site_q.astype(jnp.float32)).astype(jnp.bfloat16)
    contracted_layers = jnp.einsum("sca,vscb->vsab", site_q.astype(jnp.float32), product.astype(jnp.float32))
    sector_present = mask_q.astype(jnp.float32)
    resident_part = jnp.einsum("dixh,i->dxh", contracted_layers, sector_present * (1.0 - charge_label))
    outgoing_part = jnp.einsum("dixh,i->dxh", contracted_layers, sector_present * charge_label).astype(jnp.bfloat16)
    return resident_part, outgoing_part


def sector_psi(left_q, right_q, psi_q):
    applied = jnp.einsum("wab,vbd->wvad", left_q.astype(jnp.float32), psi_q.astype(jnp.float32)).astype(jnp.bfloat16)
    return jnp.einsum("wvad,wcd->avc", applied.astype(jnp.float32), right_q.astype(jnp.float32))


def reference(env, site_tensor, mpo, channel_mask, block_mask, state_charge, psi):
    charge_label = state_charge.astype(jnp.float32)
    results = []
    for section_index in range(2):
        weights = mpo[section_index].astype(jnp.float32) * channel_mask[section_index].astype(jnp.float32)[:, :, None]

        def per_sector(inputs):
            return sector_env(weights, charge_label, inputs[0], inputs[1], inputs[2])

        resident_part, outgoing_part = lax.map(per_sector, (jnp.moveaxis(env[section_index], 1, 0), jnp.moveaxis(site_tensor[section_index], 1, 0), block_mask[section_index].T))
        empty = jnp.zeros_like(outgoing_part[:1])
        if section_index == 0:
            shifted = jnp.concatenate([empty, outgoing_part[:-1]], axis=0)
        else:
            shifted = jnp.concatenate([outgoing_part[1:], empty], axis=0)
        advanced = (resident_part + shifted.astype(jnp.float32)).astype(jnp.bfloat16)
        results.append(jnp.moveaxis(advanced, 0, 1))
    new_env = jnp.stack(results, axis=0)

    def per_block(inputs):
        return sector_psi(inputs[0], inputs[1], inputs[2])

    applied = lax.map(per_block, (jnp.moveaxis(new_env[0], 1, 0), jnp.moveaxis(new_env[1], 1, 0), jnp.moveaxis(psi, 1, 0)))
    new_psi = jnp.transpose(applied, (1, 2, 0, 3)).astype(jnp.bfloat16)
    return new_env, new_psi
```

```python
import functools

import jax
import jax.numpy as jnp
from jax import lax
from jax.experimental import pallas as pl
from jax.experimental.pallas import tpu as pltpu
from jax.sharding import PartitionSpec as P


ROWS = 16
F32 = jnp.float32
BF16 = jnp.bfloat16


def padded(block, sides, width):
    for axis, dim in sides:
        count = lax.axis_size(axis)
        forward = [(i, i + 1) for i in range(count - 1)]
        backward = [(target, source) for source, target in forward]
        low = lax.ppermute(
            lax.slice_in_dim(block, block.shape[dim] - width, None, axis=dim), axis, forward
        )
        high = lax.ppermute(lax.slice_in_dim(block, 0, width, axis=dim), axis, backward)
        block = jnp.concatenate([low, block, high], axis=dim)
    return block


def from_partner(value, axis, bit):
    return lax.ppermute(value, axis, [(i, i ^ 1 << bit) for i in range(lax.axis_size(axis))])


def general_plan(env, site_tensor, mpo, channel_mask, block_mask, state_charge, psi):
    section = lax.axis_index("section")
    own_env = env[0]
    site_blocks = site_tensor[0]
    weights = mpo[0] * channel_mask[0].astype(BF16)[:, :, None]
    chan_dev = own_env.shape[0]
    offset_w = lax.axis_index("channel") * chan_dev
    gathered = lax.all_gather(own_env, "channel", axis=0, tiled=True)
    local_w = lax.dynamic_slice_in_dim(weights, offset_w, chan_dev, 1)
    blended = jnp.einsum(
        "wvs,wqab->vsqab", local_w, gathered, preferred_element_type=F32
    ).astype(BF16)
    product = jnp.einsum(
        "vsqac,sqcb->vsqab", blended, site_blocks, preferred_element_type=F32
    ).astype(BF16)
    layers = jnp.einsum("sqca,vsqcb->vsqab", site_blocks, product, preferred_element_type=F32)
    charge_label = state_charge.astype(F32)
    present = block_mask[0].astype(F32)
    resident = jnp.einsum("vsqab,sq->vqab", layers, present * (1.0 - charge_label)[:, None])
    outgoing = jnp.einsum("vsqab,sq->vqab", layers, present * charge_label[:, None]).astype(BF16)
    rim_cells = padded(outgoing, (("block", 1),), 1)
    sector_count = outgoing.shape[1]
    shifted = jnp.where(section == 0, rim_cells[:, :sector_count], rim_cells[:, 2:])
    new_env = (resident + shifted.astype(F32)).astype(BF16)
    partner = from_partner(new_env, "section", 0)
    left_env = jnp.where(section == 0, new_env, partner)
    right_env = jnp.where(section == 0, partner, new_env)
    applied = jnp.einsum(
        "wqab,vqbd->wvqad", left_env, psi, preferred_element_type=F32
    ).astype(BF16)
    summed = lax.psum_scatter(
        jnp.einsum("wvqad,wqcd->avqc", applied, right_env, preferred_element_type=F32),
        "channel",
        scatter_dimension=0,
        tiled=True,
    )
    return (new_env[None], summed.astype(BF16))


def dot_nn(a, b):
    return lax.dot_general(a, b, (((1,), (0,)), ((), ())), preferred_element_type=F32)


def dot_nt(a, b):
    return lax.dot_general(a, b, (((1,), (1,)), ((), ())), preferred_element_type=F32)


def sector_body(pieces_n, has_prev, has_hold, strips, sc, *refs):
    pieces = refs[:pieces_n]
    mixer, site, site_t = refs[pieces_n : pieces_n + 3]
    rest = list(refs[pieces_n + 3 :])
    prev = rest.pop(0) if has_prev else None
    hold = rest.pop(0) if has_hold else None
    first_out, second_out, mixed, prod = rest
    chan, strip, dim = pieces[0].shape
    states = site.shape[0]
    half = states // 2
    step = pl.program_id(0)

    @pl.when(step < strips)
    def _():
        for group in range(strip // ROWS):
            rows = pl.ds(group * ROWS, ROWS)
            slab = [p[:, rows, :].reshape(chan * ROWS, dim) for p in pieces]
            out = dot_nn(mixer[...], jnp.concatenate(slab, axis=0)).astype(BF16)
            mixed[:, rows, :] = out.reshape(states * chan, ROWS, dim)
        for at in range(states):
            side, k = divmod(at, half)
            left = mixed[at * chan : (at + 1) * chan].reshape(chan * strip, dim)
            out = dot_nn(left, site[sc[1 + at], 0]).astype(BF16).reshape(chan, strip, dim)
            rows = pl.ds(pl.multiple_of(k * dim + step * strip, strip), strip)
            prod[side * chan : (side + 1) * chan, rows, :] = out

    @pl.when(step >= strips)
    def _():
        v = step - strips

        def total(side):
            left = [site_t[sc[1 + side * half + k], 0] for k in range(half)]
            return dot_nn(jnp.concatenate(left, axis=1), prod[side * chan + v])

        stay = total(0)
        if has_prev:
            first_out[0] = (stay + prev[0].astype(F32)).astype(BF16)
        else:
            first_out[0] = stay
        moving = total(1).astype(BF16)
        if has_hold:
            second_out[0] = (hold[0] + moving.astype(F32)).astype(BF16)
        else:
            second_out[0] = moving


def sector_step(scalars, pieces, mixer, site, site_t, prev=None, hold=None):
    chan, dim, _ = pieces[0].shape
    states = site.shape[0]
    strip = 128
    strips = dim // strip
    by_chan = pl.BlockSpec((1, dim, dim), lambda i, sc: (jnp.maximum(i - strips, 0), 0, 0))
    in_specs = [
        pl.BlockSpec((chan, strip, dim), lambda i, sc: (0, jnp.minimum(i, strips - 1), 0))
        for _ in pieces
    ]
    in_specs += [
        pl.BlockSpec(mixer.shape, lambda i, sc: (0, 0)),
        pl.BlockSpec((states, 1, dim, dim), lambda i, sc: (0, sc[0], 0, 0)),
        pl.BlockSpec((states, 1, dim, dim), lambda i, sc: (0, sc[0], 0, 0)),
    ]
    extra = [x for x in (prev, hold) if x is not None]
    in_specs += [by_chan for _ in extra]
    body = functools.partial(sector_body, len(pieces), prev is not None, hold is not None, strips)
    flops = 2 * dim**3 * chan * states * 2 + 2 * dim * dim * mixer.shape[0] * len(pieces) * chan
    return pl.pallas_call(
        body,
        grid_spec=pltpu.PrefetchScalarGridSpec(
            num_scalar_prefetch=1,
            grid=(strips + chan,),
            in_specs=in_specs,
            out_specs=[by_chan, by_chan],
            scratch_shapes=[
                pltpu.VMEM((states * chan, strip, dim), BF16),
                pltpu.VMEM((2 * chan, states // 2 * dim, dim), BF16),
            ],
        ),
        out_shape=[
            jax.ShapeDtypeStruct((chan, dim, dim), F32 if prev is None else BF16),
            jax.ShapeDtypeStruct((chan, dim, dim), BF16),
        ],
        compiler_params=pltpu.CompilerParams(dimension_semantics=("arbitrary",)),
        cost_estimate=pl.CostEstimate(
            flops=flops, transcendentals=0, bytes_accessed=2 * dim * dim * chan * 10
        ),
    )(scalars, *pieces, mixer, site, site_t, *extra)


def ready_body(sc, other, vecs, out):
    @pl.when(sc[0] == 0)
    def _():
        for n in range(vecs.shape[0]):
            out[n, 0] = dot_nt(vecs[n], other[0]).astype(BF16)

    @pl.when(sc[0] != 0)
    def _():
        for n in range(vecs.shape[0]):
            out[n, 0] = dot_nn(other[0], vecs[n]).astype(BF16)


def ready_step(section, other, vecs):
    chan, dim, _ = other.shape
    count = vecs.shape[0]
    return pl.pallas_call(
        ready_body,
        grid_spec=pltpu.PrefetchScalarGridSpec(
            num_scalar_prefetch=1,
            grid=(chan,),
            in_specs=[
                pl.BlockSpec((1, dim, dim), lambda i, sc: (i, 0, 0)),
                pl.BlockSpec((count, dim, dim), lambda i, sc: (0, 0, 0)),
            ],
            out_specs=pl.BlockSpec((count, 1, dim, dim), lambda i, sc: (0, i, 0, 0)),
        ),
        out_shape=jax.ShapeDtypeStruct((count, chan, dim, dim), BF16),
        compiler_params=pltpu.CompilerParams(dimension_semantics=("arbitrary",)),
        cost_estimate=pl.CostEstimate(
            flops=2 * dim**3 * chan * count, transcendentals=0, bytes_accessed=2 * dim * dim * chan * 3
        ),
    )(section, other, vecs)


def apply_body(sc, own, ready, keep, send, acc):
    chan = own.shape[0]
    slots = 2 * keep.shape[0]
    rows = keep.shape[-2]

    @pl.when(sc[0] == 0)
    def _():
        total = dot_nn(own[0], ready[0, 0])
        for w in range(1, chan):
            total += dot_nn(own[w], ready[0, w])
        acc[...] = total

    @pl.when(sc[0] != 0)
    def _():
        total = dot_nt(ready[0, 0], own[0])
        for w in range(1, chan):
            total += dot_nt(ready[0, w], own[w])
        acc[...] = total

    for j in range(slots):
        start = pl.multiple_of((sc[1] ^ j) * rows, rows)
        value = acc[pl.ds(start, rows), :]
        if j % 2:
            send[j // 2, 0] = value.astype(BF16)
        else:
            keep[j // 2, 0] = value


def apply_step(scalars, own, ready, slots):
    chan, dim, _ = own.shape
    count = ready.shape[0]
    shape = (slots // 2, count, dim // slots, dim)
    spec = pl.BlockSpec((slots // 2, 1, dim // slots, dim), lambda n, sc: (0, n, 0, 0))
    return pl.pallas_call(
        apply_body,
        grid_spec=pltpu.PrefetchScalarGridSpec(
            num_scalar_prefetch=1,
            grid=(count,),
            in_specs=[
                pl.BlockSpec((chan, dim, dim), lambda n, sc: (0, 0, 0)),
                pl.BlockSpec((1, chan, dim, dim), lambda n, sc: (n, 0, 0, 0)),
            ],
            out_specs=[spec, spec],
            scratch_shapes=[pltpu.VMEM((dim, dim), F32)],
        ),
        out_shape=[jax.ShapeDtypeStruct(shape, F32), jax.ShapeDtypeStruct(shape, BF16)],
        compiler_params=pltpu.CompilerParams(dimension_semantics=("arbitrary",)),
        cost_estimate=pl.CostEstimate(
            flops=2 * dim**3 * chan * count, transcendentals=0, bytes_accessed=2 * dim * dim * chan * 3
        ),
    )(scalars, own, ready)


def place_body(sc, *refs):
    out = refs[-1]
    for u, part in enumerate(refs[:-1]):
        out[0, pl.ds(sc[u], 1)] = part[...]


def place_step(slots, parts):
    chan, dim, _ = parts[0].shape
    return pl.pallas_call(
        place_body,
        grid_spec=pltpu.PrefetchScalarGridSpec(
            num_scalar_prefetch=1,
            grid=(chan,),
            in_specs=[pl.BlockSpec((1, dim, dim), lambda i, sc: (i, 0, 0)) for _ in parts],
            out_specs=pl.BlockSpec((1, len(parts), dim, dim), lambda i, sc: (i, 0, 0, 0)),
        ),
        out_shape=jax.ShapeDtypeStruct((chan, len(parts), dim, dim), parts[0].dtype),
        compiler_params=pltpu.CompilerParams(dimension_semantics=("arbitrary",)),
    )(slots, *parts)


def swap(value, axis, bit=0):
    return lax.ppermute(value, axis, [(i, i ^ (1 << bit)) for i in range(lax.axis_size(axis))])


def pick(array, index, axis):
    return lax.dynamic_index_in_dim(array, index, axis, keepdims=False)


def sector_order(sectors):
    return [sectors - 1] + list(range(sectors - 1))


def pipelined_plan(env, site_tensor, mpo, channel_mask, block_mask, state_charge, psi):
    section = lax.axis_index("section")
    me = lax.axis_index("channel")
    peers = lax.axis_size("channel")
    bits = peers.bit_length() - 1
    blocks = lax.axis_size("block")
    own_env = env[0]
    chan, sectors, _, _ = own_env.shape
    site = site_tensor[0]
    states = site.shape[0]

    def sector(u):
        return jnp.where(section == 0, u, sectors - 1 - u)

    order = sector_order(sectors)

    gathered = {}
    for u in order:
        pieces = {0: lax.optimization_barrier(pick(own_env, sector(u), 1))}
        for bit in reversed(range(bits)):
            moved = {}
            for j, p in pieces.items():
                moved[j | 1 << bit] = swap(p, "channel", bit)
            pieces.update(moved)
        gathered[u] = [pieces[j] for j in range(peers)]

    upper = range(sectors // 2, sectors)
    vecs = {}
    for u in upper:
        mine = pick(psi[0], sector(u), 0)
        theirs = swap(pick(psi[0], sector(sectors - 1 - u), 0), "section")
        vecs[u] = jnp.stack([mine, theirs])

    inputs = peers * chan
    outputs = states * chan
    key = state_charge * states + jnp.arange(states, dtype=jnp.int32)
    rank = jnp.sum((key[None, :] < key[:, None]).astype(jnp.int32), axis=1)
    chosen = rank[None, :] == jnp.arange(states, dtype=jnp.int32)[:, None]
    state_ids = jnp.arange(states, dtype=jnp.int32)[None, :]
    state_order = jnp.sum(jnp.where(chosen, state_ids, 0), axis=1)
    weights = mpo[0].astype(F32) * channel_mask[0].astype(F32)[:, :, None]
    weights = lax.dynamic_slice_in_dim(weights, me * chan, chan, 1)
    weights = weights.reshape(peers, chan, chan, states)
    weights = jnp.stack([pick(weights, me ^ j, 0) for j in range(peers)])
    weights = weights.reshape(inputs, chan, states)
    out_row = jnp.arange(outputs * ROWS)[:, None]
    in_row = jnp.arange(inputs * ROWS)[None, :]
    spread_out = (out_row // ROWS == jnp.arange(outputs)[None, :]).astype(BF16)
    spread_in = (in_row // ROWS == jnp.arange(inputs)[:, None]).astype(BF16)
    same_row = out_row % ROWS == in_row % ROWS
    site_t = jnp.swapaxes(site, 2, 3)

    def mixer(u):
        present = pick(block_mask[0], sector(u), 1).astype(F32)
        by_state = jnp.moveaxis(weights * present, 2, 0)
        picked = jnp.where(chosen[:, :, None, None], by_state[None], 0.0)
        table = jnp.swapaxes(jnp.sum(picked, axis=1), 1, 2).reshape(outputs, inputs)
        wide = spread_out @ table.astype(BF16) @ spread_in
        return jnp.where(same_row, wide, 0).astype(BF16)

    def scalars(u):
        return jnp.concatenate([sector(u)[None], state_order]).astype(jnp.int32)

    def step(u, *extra):
        return sector_step(scalars(u), gathered[u], mixer(u), site, site_t, *extra)

    links = [(b, b + 1) for b in range(blocks - 1)]
    links += [(blocks + b + 1, blocks + b) for b in range(blocks - 1)]

    new = {}
    last = sectors - 1
    hold, moving = step(last)
    raised = lax.ppermute(moving, ("section", "block"), links)
    for u in range(last):
        final = hold if u == last - 1 else None
        new[u], moving = step(u, moving if u else None, final)
        if u == 0:
            new[0] = (new[0] + raised.astype(F32)).astype(BF16)
    new[last] = moving

    flag = section.astype(jnp.int32)[None]
    ready = {}
    for u in reversed(upper):
        other = swap(new[sectors - 1 - u], "section")
        ready[u] = ready_step(flag, other, vecs[u])

    where = jnp.stack([section, me]).astype(jnp.int32)
    done = {}
    for u in reversed(upper):
        keep, send = apply_step(where, new[u], ready[u], peers)
        keep = keep + swap(send, "channel", 0).astype(F32)
        for bit in range(1, bits):
            pairs = keep.reshape((keep.shape[0] // 2, 2) + keep.shape[1:])
            keep = pairs[:, 0] + swap(pairs[:, 1].astype(BF16), "channel", bit).astype(F32)
        done[u] = (keep[0, 0].astype(BF16), swap(keep[0, 1].astype(BF16), "section"))

    blocks_q = [done[last - i][1] for i in range(sectors // 2)] + [done[u][0] for u in upper]
    ordered = jnp.stack(blocks_q, axis=1)
    new_psi = jnp.where(section == 0, ordered, jnp.flip(ordered, 1))[:, None]
    slots = jnp.stack([sector(u) for u in range(sectors)]).astype(jnp.int32)
    new_env = place_step(slots, [new[u] for u in range(sectors)])
    return (new_env[None], new_psi)


def is_pipelined(peers, chan, sectors, dim, states):
    return (
        peers > 1
        and peers & (peers - 1) == 0
        and sectors % 2 == 0
        and dim % 128 == 0
        and dim % (8 * peers) == 0
        and peers * chan * ROWS <= 512
        and states * chan * ROWS <= 512
    )


def per_device(env, site_tensor, mpo, channel_mask, block_mask, state_charge, psi):
    args = (env, site_tensor, mpo, channel_mask, block_mask, state_charge, psi)
    chan, sectors, dim = env.shape[1:4]
    peers = lax.axis_size("channel")
    if is_pipelined(peers, chan, sectors, dim, site_tensor.shape[1]):
        return pipelined_plan(*args)
    return general_plan(*args)


def solution(mesh):
    return jax.shard_map(
        per_device,
        mesh=mesh,
        in_specs=(
            P("section", "channel", "block", None, None),
            P("section", None, "block", None, None),
            P("section", None, None, None),
            P("section", None, None),
            P("section", None, "block"),
            P(),
            P("section", "block", None, None),
        ),
        out_specs=(
            P("section", "channel", "block", None, None),
            P("channel", "section", "block", None),
        ),
        check_vma=False,
    )
```

```python
import functools

import jax
import jax.numpy as jnp
from jax import lax
from jax.experimental import pallas as pl
from jax.experimental.pallas import tpu as pltpu
from jax.sharding import PartitionSpec as P


ROWS = 16
F32 = jnp.float32
BF16 = jnp.bfloat16


def padded(block, sides, width):
    for axis, dim in sides:
        count = lax.axis_size(axis)
        forward = [(i, i + 1) for i in range(count - 1)]
        backward = [(target, source) for source, target in forward]
        low = lax.ppermute(
            lax.slice_in_dim(block, block.shape[dim] - width, None, axis=dim), axis, forward
        )
        high = lax.ppermute(lax.slice_in_dim(block, 0, width, axis=dim), axis, backward)
        block = jnp.concatenate([low, block, high], axis=dim)
    return block


def from_partner(value, axis, bit):
    return lax.ppermute(value, axis, [(i, i ^ 1 << bit) for i in range(lax.axis_size(axis))])


def general_plan(env, site_tensor, mpo, channel_mask, block_mask, state_charge, psi):
    section = lax.axis_index("section")
    own_env = env[0]
    site_blocks = site_tensor[0]
    weights = mpo[0] * channel_mask[0].astype(BF16)[:, :, None]
    chan_dev = own_env.shape[0]
    offset_w = lax.axis_index("channel") * chan_dev
    gathered = lax.all_gather(own_env, "channel", axis=0, tiled=True)
    local_w = lax.dynamic_slice_in_dim(weights, offset_w, chan_dev, 1)
    blended = jnp.einsum(
        "wvs,wqab->vsqab", local_w, gathered, preferred_element_type=F32
    ).astype(BF16)
    product = jnp.einsum(
        "vsqac,sqcb->vsqab", blended, site_blocks, preferred_element_type=F32
    ).astype(BF16)
    layers = jnp.einsum("sqca,vsqcb->vsqab", site_blocks, product, preferred_element_type=F32)
    charge_label = state_charge.astype(F32)
    present = block_mask[0].astype(F32)
    resident = jnp.einsum("vsqab,sq->vqab", layers, present * (1.0 - charge_label)[:, None])
    outgoing = jnp.einsum("vsqab,sq->vqab", layers, present * charge_label[:, None]).astype(BF16)
    rim_cells = padded(outgoing, (("block", 1),), 1)
    sector_count = outgoing.shape[1]
    shifted = jnp.where(section == 0, rim_cells[:, :sector_count], rim_cells[:, 2:])
    new_env = (resident + shifted.astype(F32)).astype(BF16)
    partner = from_partner(new_env, "section", 0)
    left_env = jnp.where(section == 0, new_env, partner)
    right_env = jnp.where(section == 0, partner, new_env)
    applied = jnp.einsum(
        "wqab,vqbd->wvqad", left_env, psi, preferred_element_type=F32
    ).astype(BF16)
    summed = lax.psum_scatter(
        jnp.einsum("wvqad,wqcd->avqc", applied, right_env, preferred_element_type=F32),
        "channel",
        scatter_dimension=0,
        tiled=True,
    )
    return (new_env[None], summed.astype(BF16))


def dot_nn(a, b):
    return lax.dot_general(a, b, (((1,), (0,)), ((), ())), preferred_element_type=F32)


def dot_nt(a, b):
    return lax.dot_general(a, b, (((1,), (1,)), ((), ())), preferred_element_type=F32)


VMEM = pl.BlockSpec(memory_space=pltpu.VMEM)
SMEM = pl.BlockSpec(memory_space=pltpu.SMEM)
HBM = pl.BlockSpec(memory_space=pltpu.HBM)


def in_hbm(array):
    return pltpu.with_memory_space_constraint(array, pltpu.HBM)


def pick_body(start, index, array, out, sem):
    rows = pl.ds(start, out.shape[1])
    copy = pltpu.make_async_copy(array.at[:, index[0], rows], out, sem)
    copy.start()
    copy.wait()


def pick_block(array, index, start, rows):
    lead, _, _, cols = array.shape
    return pl.pallas_call(
        functools.partial(pick_body, start),
        in_specs=[SMEM, HBM],
        out_specs=VMEM,
        out_shape=jax.ShapeDtypeStruct((lead, rows, cols), array.dtype),
        scratch_shapes=[pltpu.SemaphoreType.DMA],
        compiler_params=pltpu.CompilerParams(vmem_limit_bytes=4 << 20),
    )(index[None].astype(jnp.int32), in_hbm(array))


def turn_body(sc, site, plain, turned, blocks, flips, sems):
    count = blocks.shape[0]
    loads = [
        pltpu.make_async_copy(site.at[sc[1 + s], sc[0]], blocks.at[s], sems.at[0, s]) for s in range(count)
    ]
    for load in loads:
        load.start()
    stores = []
    for s in range(count):
        loads[s].wait()
        stores.append(pltpu.make_async_copy(blocks.at[s], plain.at[s], sems.at[1, s]))
        stores[-1].start()
        flips[s] = blocks[s].T
        stores.append(pltpu.make_async_copy(flips.at[s], turned.at[s], sems.at[2, s]))
        stores[-1].start()
    for store in stores:
        store.wait()


def turn_blocks(scalars, site):
    states, _, dim, _ = site.shape
    shape = pltpu.HBM((states, dim, dim), site.dtype)
    return pl.pallas_call(
        turn_body,
        in_specs=[SMEM, HBM],
        out_specs=[HBM, HBM],
        out_shape=[shape, shape],
        scratch_shapes=[
            pltpu.VMEM((states, dim, dim), site.dtype),
            pltpu.VMEM((states, dim, dim), site.dtype),
            pltpu.SemaphoreType.DMA((3, states)),
        ],
        compiler_params=pltpu.CompilerParams(vmem_limit_bytes=8 << 20),
    )(scalars, in_hbm(site))


def sector_body(plan, *refs):
    peers, groups_n, start, sides = plan
    refs = list(refs)
    groups = [[refs.pop(0) for _ in range(peers)] for _ in range(groups_n)]
    mixer, site, site_t = [refs.pop(0) for _ in range(3)]
    adds = [[refs.pop(0) if used else None for used in side[1:3]] for side in sides]
    outs = [refs.pop(0) for _ in sides]
    mixed, prod = refs
    chan, _, dim = groups[0][0].shape
    total = sum(group[0].shape[1] for group in groups)
    half = site.shape[0] // 2
    per_side = half * chan
    lead = sides[0][0] * per_side * ROWS
    weight = mixer[lead : lead + len(sides) * per_side * ROWS, :]

    def mix(pieces, strip, ahead, step, carry):
        first_row = pl.multiple_of(step * strip, strip)
        for group in range(strip // ROWS):
            at = pl.ds(first_row + group * ROWS, ROWS)
            slab = jnp.concatenate([p[:, at, :].reshape(chan * ROWS, dim) for p in pieces], axis=0)
            out = dot_nn(weight, slab).astype(BF16)
            mixed[:, pl.ds(group * ROWS, ROWS), :] = out.reshape(len(sides) * per_side, ROWS, dim)
        for n, (side, *_) in enumerate(sides):
            for k in range(half):
                first = n * per_side + k * chan
                left = mixed[first : first + chan, :strip].reshape(chan * strip, dim)
                out = dot_nn(left, site[side * half + k]).astype(BF16).reshape(chan, strip, dim)
                at = pl.ds(pl.multiple_of(k * total + ahead + first_row, 128), strip)
                prod[n * chan : (n + 1) * chan, at, :] = out
        return carry

    ahead = 0
    for pieces in groups:
        rows = pieces[0].shape[1]
        strip = strip_of(rows)
        lax.fori_loop(0, rows // strip, functools.partial(mix, pieces, strip, ahead), 0)
        ahead += rows

    def join(v, carry):
        for n, (side, _, _, wide) in enumerate(sides):
            left = [site_t[side * half + k, :, start : start + total] for k in range(half)]
            value = dot_nn(jnp.concatenate(left, axis=1), prod[n * chan + v])
            base, late = adds[n]
            if base is not None:
                value += base[v]
            if side == 1 and not wide:
                value = value.astype(BF16).astype(F32)
            if late is not None:
                value += late[v].astype(F32)
            outs[n][v] = value.astype(F32 if wide else BF16)
        return carry

    lax.fori_loop(0, chan, join, 0)


def strip_of(rows):
    return 256 if rows % 256 == 0 else 128


def sector_step(groups, mixer, site, site_t, start, sides):
    chan, _, dim = groups[0][0].shape
    rows = [group[0].shape[1] for group in groups]
    total = sum(rows)
    strip = max(strip_of(r) for r in rows)
    half = site.shape[0] // 2
    count = len(sides)
    peers = len(groups[0])
    extra = [x for side in sides for x in side[1:3] if x is not None]
    marks = tuple((side, base is not None, late is not None, wide) for side, base, late, wide in sides)
    return pl.pallas_call(
        functools.partial(sector_body, (peers, len(groups), start, marks)),
        in_specs=[VMEM] * (len(groups) * peers + 3 + len(extra)),
        out_specs=[VMEM] * count,
        out_shape=[jax.ShapeDtypeStruct((chan, dim, dim), F32 if side[3] else BF16) for side in sides],
        scratch_shapes=[
            pltpu.VMEM((count * half * chan, strip, dim), BF16),
            pltpu.VMEM((count * chan, half * total, dim), BF16),
        ],
        compiler_params=pltpu.CompilerParams(vmem_limit_bytes=STEP_LIMIT),
        cost_estimate=pl.CostEstimate(
            flops=4 * dim * dim * total * chan * half * count,
            transcendentals=0,
            bytes_accessed=2 * dim * total * chan * 8,
        ),
    )(*[piece for group in groups for piece in group], mixer, site, site_t, *extra)


STEP_LIMIT = 40 << 20


def ready_body(flag, other, mine, theirs, out):
    def each(w, carry):
        for n, vec in enumerate((mine, theirs)):

            @pl.when(flag[0] == 0)
            def _():
                out[n, w] = dot_nt(vec[...], other[w]).astype(BF16)

            @pl.when(flag[0] != 0)
            def _():
                out[n, w] = dot_nn(other[w], vec[...]).astype(BF16)

        return carry

    lax.fori_loop(0, other.shape[0], each, 0)


def ready_step(section, other, vecs):
    chan, dim, _ = other.shape
    return pl.pallas_call(
        ready_body,
        in_specs=[SMEM, VMEM, VMEM, VMEM],
        out_specs=VMEM,
        out_shape=jax.ShapeDtypeStruct((2, chan, dim, dim), BF16),
        compiler_params=pltpu.CompilerParams(vmem_limit_bytes=STEP_LIMIT),
        cost_estimate=pl.CostEstimate(
            flops=4 * dim**3 * chan, transcendentals=0, bytes_accessed=2 * dim * dim * chan * 3
        ),
    )(section, other, *vecs)


def apply_body(n, sc, own, ready, keep, send, acc):
    chan = own.shape[0]
    rows = keep.shape[-2]

    @pl.when(sc[0] == 0)
    def _():
        total = dot_nn(own[0], ready[n, 0])
        for w in range(1, chan):
            total += dot_nn(own[w], ready[n, w])
        acc[...] = total

    @pl.when(sc[0] != 0)
    def _():
        total = dot_nt(ready[n, 0], own[0])
        for w in range(1, chan):
            total += dot_nt(ready[n, w], own[w])
        acc[...] = total

    for j in range(2 * keep.shape[0]):
        start = pl.multiple_of((sc[1] ^ j) * rows, rows)
        value = acc[pl.ds(start, rows), :]
        if j % 2:
            send[j // 2] = value.astype(BF16)
        else:
            keep[j // 2] = value


def apply_step(n, scalars, own, ready, slots):
    chan, dim, _ = own.shape
    shape = (slots // 2, dim // slots, dim)
    return pl.pallas_call(
        functools.partial(apply_body, n),
        in_specs=[SMEM, VMEM, VMEM],
        out_specs=[VMEM, VMEM],
        out_shape=[jax.ShapeDtypeStruct(shape, F32), jax.ShapeDtypeStruct(shape, BF16)],
        scratch_shapes=[pltpu.VMEM((dim, dim), F32)],
        compiler_params=pltpu.CompilerParams(vmem_limit_bytes=STEP_LIMIT),
        cost_estimate=pl.CostEstimate(
            flops=2 * dim**3 * chan, transcendentals=0, bytes_accessed=2 * dim * dim * chan * 3
        ),
    )(scalars, own, ready)


def place_body(count, slots, *refs):
    out, sems = refs[-2:]
    copies = [
        pltpu.make_async_copy(refs[u], out.at[:, slots[u]], sems.at[u]) for u in range(count)
    ]
    for copy in copies:
        copy.start()
    for copy in copies:
        copy.wait()


def place_step(slots, parts, sectors, onto=None):
    chan, dim, _ = parts[0].shape
    count = len(parts)
    extra = [] if onto is None else [onto]
    return pl.pallas_call(
        functools.partial(place_body, count),
        in_specs=[SMEM] + [VMEM] * count + [HBM] * len(extra),
        out_specs=HBM,
        out_shape=jax.ShapeDtypeStruct((chan, sectors, dim, dim), parts[0].dtype),
        scratch_shapes=[pltpu.SemaphoreType.DMA((count,))],
        input_output_aliases={1 + count: 0} if extra else {},
        compiler_params=pltpu.CompilerParams(vmem_limit_bytes=4 << 20),
    )(slots, *parts, *extra)


def swap(value, axis, bit=0):
    return lax.ppermute(value, axis, [(i, i ^ (1 << bit)) for i in range(lax.axis_size(axis))])


def pick(array, index, axis):
    return lax.dynamic_index_in_dim(array, index, axis, keepdims=False)


def sector_order(sectors):
    return [sectors - 1] + list(range(sectors - 1))


def pipelined_plan(env, site_tensor, mpo, channel_mask, block_mask, state_charge, psi):
    section = lax.axis_index("section")
    me = lax.axis_index("channel")
    peers = lax.axis_size("channel")
    bits = peers.bit_length() - 1
    blocks = lax.axis_size("block")
    own_env = env[0]
    chan, sectors, dim, _ = own_env.shape
    site = site_tensor[0]
    states = site.shape[0]

    def sector(u):
        return jnp.where(section == 0, u, sectors - 1 - u)

    order = sector_order(sectors)

    def gather(u, start, rows):
        pieces = {0: pick_block(own_env, sector(u), start, rows)}
        for bit in reversed(range(bits)):
            moved = {}
            for j, p in pieces.items():
                moved[j | 1 << bit] = swap(p, "channel", bit)
            pieces.update(moved)
        return [pieces[j] for j in range(peers)]

    split = split_rows(dim)
    gathered = {}
    for u in order:
        if u in (order[0], order[-1]):
            gathered[u] = [gather(u, 0, split), gather(u, split, dim - split)]
        else:
            gathered[u] = [gather(u, 0, dim)]

    upper = range(sectors // 2, sectors)
    vecs = {}
    for u in upper:
        mine = pick(psi[0], sector(u), 0)
        theirs = swap(pick(psi[0], sector(sectors - 1 - u), 0), "section")
        vecs[u] = (mine, theirs)

    inputs = peers * chan
    outputs = states * chan
    key = state_charge * states + jnp.arange(states, dtype=jnp.int32)
    rank = jnp.sum((key[None, :] < key[:, None]).astype(jnp.int32), axis=1)
    chosen = rank[None, :] == jnp.arange(states, dtype=jnp.int32)[:, None]
    state_ids = jnp.arange(states, dtype=jnp.int32)[None, :]
    state_order = jnp.sum(jnp.where(chosen, state_ids, 0), axis=1)
    weights = mpo[0].astype(F32) * channel_mask[0].astype(F32)[:, :, None]
    weights = lax.dynamic_slice_in_dim(weights, me * chan, chan, 1)
    weights = weights.reshape(peers, chan, chan, states)
    weights = jnp.stack([pick(weights, me ^ j, 0) for j in range(peers)])
    weights = weights.reshape(inputs, chan, states)
    out_row = jnp.arange(outputs * ROWS)[:, None]
    in_row = jnp.arange(inputs * ROWS)[None, :]
    spread_out = (out_row // ROWS == jnp.arange(outputs)[None, :]).astype(BF16)
    spread_in = (in_row // ROWS == jnp.arange(inputs)[:, None]).astype(BF16)
    same_row = out_row % ROWS == in_row % ROWS

    def mixer(u):
        present = pick(block_mask[0], sector(u), 1).astype(F32)
        by_state = jnp.moveaxis(weights * present, 2, 0)
        picked = jnp.where(chosen[:, :, None, None], by_state[None], 0.0)
        table = jnp.swapaxes(jnp.sum(picked, axis=1), 1, 2).reshape(outputs, inputs)
        wide = spread_out @ table.astype(BF16) @ spread_in
        return jnp.where(same_row, wide, 0).astype(BF16)

    def scalars(u):
        return jnp.concatenate([sector(u)[None], state_order]).astype(jnp.int32)

    turned = {}
    for u in order:
        scalar = scalars(u)
        turned[u] = turn_blocks(scalar, site)

    def step(u, groups, start, *sides):
        return sector_step(groups, mixer(u), *turned[u], start, sides)

    links = [(b, b + 1) for b in range(blocks - 1)]
    links += [(blocks + b + 1, blocks + b) for b in range(blocks - 1)]

    new = {}
    last, end = order[0], order[-1]
    early, late = ([group] for group in gathered[last])
    [part] = step(last, early, 0, (1, None, None, True))
    [moving] = step(last, late, split, (1, part, None, False))
    raised = lax.ppermute(moving, ("section", "block"), links)
    [hold] = step(last, gathered[last], 0, (0, None, None, True))
    for u in order[1:-1]:
        if u == 0:
            [stay] = step(u, gathered[u], 0, (0, None, None, True))
            new[u] = (stay + raised.astype(F32)).astype(BF16)
            [moving] = step(u, gathered[u], 0, (1, None, None, False))
        else:
            new[u], moving = step(
                u, gathered[u], 0, (0, None, moving, False), (1, None, None, False)
            )
    early, late = ([group] for group in gathered[end])
    parts = step(end, early, 0, (0, None, None, True), (1, None, None, True))
    new[end], new[last] = step(
        end, late, split, (0, parts[0], moving, False), (1, parts[1], hold, False)
    )

    flag = section.astype(jnp.int32)[None]
    ready = {}
    for u in reversed(upper):
        other = swap(new[sectors - 1 - u], "section")
        ready[u] = ready_step(flag, other, vecs[u])

    where = jnp.stack([section, me]).astype(jnp.int32)
    done = {}
    for u in reversed(upper):
        ends = []
        for n in (1, 0):
            keep, send = apply_step(n, where, new[u], ready[u], peers)
            keep = keep + swap(send, "channel", 0).astype(F32)
            for bit in range(1, bits):
                pairs = keep.reshape((keep.shape[0] // 2, 2) + keep.shape[1:])
                keep = pairs[:, 0] + swap(pairs[:, 1].astype(BF16), "channel", bit).astype(F32)
            ends.append(keep[0].astype(BF16))
        done[u] = (ends[1], swap(ends[0], "section"))

    blocks_q = [done[last - i][1] for i in range(sectors // 2)] + [done[u][0] for u in upper]
    ordered = jnp.stack(blocks_q, axis=1)
    new_psi = jnp.where(section == 0, ordered, jnp.flip(ordered, 1))[:, None]
    new_env = None
    for us in (order[1:-1], [order[-1], order[0]]):
        slots = jnp.stack([sector(u) for u in us]).astype(jnp.int32)
        new_env = place_step(slots, [new[u] for u in us], sectors, new_env)
    return (new_env[None], new_psi)


def split_rows(dim):
    return dim // 4 * 3


def is_pipelined(peers, chan, sectors, dim, states):
    return (
        peers > 1
        and peers & (peers - 1) == 0
        and sectors % 2 == 0
        and sectors == 4
        and peers == 4
        and states % 2 == 0
        and dim % 512 == 0
        and dim % (8 * peers) == 0
        and peers * chan * ROWS <= 512
        and states * chan * ROWS <= 512
    )


def per_device(env, site_tensor, mpo, channel_mask, block_mask, state_charge, psi):
    args = (env, site_tensor, mpo, channel_mask, block_mask, state_charge, psi)
    chan, sectors, dim = env.shape[1:4]
    peers = lax.axis_size("channel")
    if is_pipelined(peers, chan, sectors, dim, site_tensor.shape[1]):
        return pipelined_plan(*args)
    return general_plan(*args)


def solution(mesh):
    return jax.shard_map(
        per_device,
        mesh=mesh,
        in_specs=(
            P("section", "channel", "block", None, None),
            P("section", None, "block", None, None),
            P("section", None, None, None),
            P("section", None, None),
            P("section", None, "block"),
            P(),
            P("section", "block", None, None),
        ),
        out_specs=(
            P("section", "channel", "block", None, None),
            P("channel", "section", "block", None),
        ),
        check_vma=False,
    )
```
